32 devices in a mesh: occi: 4 (over y, core), occj: 8 (over z, x).
Axes of the slice: x: 2, y: 2, z: 4, core: 2. Of those that a mesh axis runs over, the one named last changes fastest.
Arguments:
- factors: float32 [32, 512, 256], P(('occi', 'occj')), may hold values from -6 to 6
- pno_vecs: float32 [2048, 256, 128], P(('occi', 'occj')), may hold values from -0.09375 to 0.09375
- pair_occ: int32 [2048, 2], P(('occi', 'occj')), may hold values from 0 to 31, as said below
- pno_count: int32 [2048], P(('occi', 'occj')), may hold values from 32 to 128, as said below
- pno_energy: float32 [2048, 128], P(('occi', 'occj')), may hold values from 0.3 to 3
- occ_energy: float32 [32], replicated, may hold values from -1.5 to -0.3
- coupi_peer: int32 [1024, 1], P(('occi', 'occj')), may hold values from 0 to 3; in each aligned block of 32 rows (0 to 31, 32 to 63, ...) at most 16 rows name the same one
- coupi_slot: int32 [1024], P(('occi', 'occj')), may hold values from 0 to 63
- coupi_target: int32 [1024], P(('occi', 'occj')), may hold values from 0 to 63
- coupi_fock: float32 [1024], P(('occi', 'occj')), may hold values from -0.5 to 0.5
- coupi_correlation: float32 [1024, 128, 128], P(('occi', 'occj')), may hold values from -0.15 to 1, as said below
- coupj_peer: int32 [1024, 1], P(('occi', 'occj')), may hold values from 0 to 7; in each aligned block of 32 rows (0 to 31, 32 to 63, ...) at most 8 rows name the same one
- coupj_slot: int32 [1024], P(('occi', 'occj')), may hold values from 0 to 63
- coupj_target: int32 [1024], P(('occi', 'occj')), may hold values from 0 to 63
- coupj_fock: float32 [1024], P(('occi', 'occj')), may hold values from -0.5 to 0.5
- coupj_correlation: float32 [1024, 128, 128], P(('occi', 'occj')), may hold values from -0.15 to 1, as said below
Outputs:
- amplitude: float32 [2048, 128, 128], P(('occi', 'occj'))
- residual: float32 [2048, 128, 128], P(('occi', 'occj'))
The draws below stay inside these ranges and needn't reach their ends.
Inputs may be any that keep to these rules, and one draw needn't show every extreme that they name: `pair_occ`: the pairs in the rows of one device have their first orbital in that device's occi block of 1 * 8 orbitals starting at u * 8, and their second orbital o in its occj block: (o) % 8 equals the device's occj index. `pno_count`: pair 0 uses all 128 natural orbitals. `coupi_peer`: in the rows of one device no peer index appears more than 16 times. `coupj_peer`: in the rows of one device no peer index appears more than 8 times. `coupi_correlation`: diagonal entries lie in 0.5 to 1. `coupj_correlation`: diagonal entries lie in 0.5 to 1.
All inputs are finite; a program needn't handle non-finite values.
Results may differ from the reference program's by a relative error of at most 0.0003.
Values sent between devices are 32-bit elements; how exact they have to be, the bound alone decides.
No kernel may reach another device: no remote copies, remote signals or barrier semaphores. Data moves between devices by JAX's collectives and lax.ppermute only.
A program may use at most 128 MiB of HBM per device.

```python
import math
import jax
import jax.numpy as jnp
import numpy as np
from jax import lax

NAUX = 512
NVIR = 256
NPNO = 128
OCC_DEV = 1
PAIRS_DEV = 64
COUPI_DEV = 32
COUPJ_DEV = 32
ITERS = 2
CAPI = 16
CAPJ = 8
NOCC = 32
PAIRS = 2048
COUPI = 1024
COUPJ = 1024
N_OCCI = 4
N_OCCJ = 8


def draw_pair_occ(key, part):
    device_count = N_OCCI * N_OCCJ
    block_first = OCC_DEV * N_OCCJ
    block_second = OCC_DEV * N_OCCI
    cell_count = block_first * block_second
    repeats = (PAIRS_DEV + cell_count - 1) // cell_count
    device_keys = jax.random.split(jax.random.fold_in(key, 11), device_count)

    def choose(device_key):
        shuffled = jax.random.permutation(device_key, cell_count * repeats)
        return shuffled[:PAIRS_DEV] % cell_count
    chosen = jax.vmap(choose)(device_keys)
    device = jnp.arange(device_count)[:, None]
    first_block = device // N_OCCJ
    second_block = device % N_OCCJ
    row_first = chosen // block_second
    row_second = chosen % block_second
    occ_first = first_block * block_first + row_first
    occ_second = (row_second // OCC_DEV * N_OCCJ + second_block) * OCC_DEV + row_second % OCC_DEV
    return jnp.stack([occ_first, occ_second], -1).reshape(device_count * PAIRS_DEV, 2).astype(jnp.int32)


def draw_pno_count(key, part):
    counts = jax.random.randint(jax.random.fold_in(key, 13), (PAIRS_DEV * N_OCCI * N_OCCJ,), NPNO // 4, NPNO + 1)
    return counts.at[0].set(NPNO).astype(jnp.int32)


def correlation_draw(key, count):
    diagonal = jax.random.uniform(jax.random.fold_in(key, 1), (count, NPNO), jnp.float32, 0.5, 1.0)
    spread = jnp.clip(0.03 * jax.random.normal(jax.random.fold_in(key, 2), (count, NPNO, NPNO), jnp.float32), -0.15, 0.15)
    eye = jnp.eye(NPNO, dtype=jnp.float32)
    return (spread * (1.0 - eye) + diagonal[:, :, None] * eye).astype(jnp.float32)


def draw_coupi_correlation(key, part):
    return correlation_draw(jax.random.fold_in(key, 21), COUPI_DEV * N_OCCI * N_OCCJ)


def draw_coupj_correlation(key, part):
    return correlation_draw(jax.random.fold_in(key, 23), COUPJ_DEV * N_OCCI * N_OCCJ)


def with_ends(array, own_key, least, top_value):
    place = [jax.random.randint(jax.random.fold_in(own_key, axis), (), 0, length) for axis, length in enumerate(array.shape)]
    longest = array.shape.index(max(array.shape))
    neighbour = place[:longest] + [(place[longest] + 1) % array.shape[longest]] + place[longest + 1:]
    return array.at[tuple(place)].set(least).at[tuple(neighbour)].set(top_value)


def shard_levels(key, extent, shards, least, largest):
    factor_of = 1.0
    for axis_at, parts in shards:
        steps = jax.random.uniform(jax.random.fold_in(jax.random.fold_in(key, 6), axis_at), (parts,), jnp.float32, least / len(shards), largest / len(shards))
        factor_of = factor_of * jnp.repeat(jnp.exp(steps), extent[axis_at] // parts).reshape((-1,) + (1,) * (len(extent) - 1 - axis_at))
    return factor_of


def shared_out(rng, own, number, rows, number_of, top, bound, skew):
    ranking = jax.random.permutation(rng, number_of)
    heavy_load, common = load_shares(number_of, rows * top, bound, skew, True), load_shares(number_of, rows * top, bound, skew, False)
    places = jnp.arange(number_of)

    def named(tallies, turn):
        used = int((tallies > 0).sum())
        fixed = max(1, used // 4)
        shifted = fixed + (places - fixed + turn * (used - fixed)) % max(1, number_of - fixed)
        return jnp.zeros((number_of,), jnp.int32).at[ranking[jnp.where(places < fixed, places, shifted)]].set(jnp.asarray(tallies, jnp.int32))

    tallies = jnp.where(number % 4 == 0, named(heavy_load, number // 4), named(common, number - number // 4 - 1))
    mixed = jax.random.permutation(jax.random.fold_in(own, 3), number_of)
    source_of, receiver = mixed[0:number_of // 2 * 2:2], mixed[1:number_of // 2 * 2:2]
    room = jnp.minimum(tallies[source_of] - 1, bound - tallies[receiver]) // 2
    room = jnp.where((source_of == ranking[0]) | (receiver == ranking[0]) | (tallies[receiver] == 0), 0, jnp.maximum(room, 0))
    shifted = jax.random.randint(jax.random.fold_in(own, 4), (number_of // 2,), 0, 1 << 20) % (room + 1)
    tallies = tallies.at[source_of].add(-shifted).at[receiver].add(shifted)
    members = jnp.searchsorted(jnp.cumsum(tallies), jnp.arange(rows * top), side="right").astype(jnp.int32)
    listing = members.reshape(top, rows).T
    listing = listing[jax.random.permutation(jax.random.fold_in(own, 1), rows)]
    turn = jax.random.randint(jax.random.fold_in(own, 2), (rows, 1), 0, top)
    return jnp.take_along_axis(listing, (jnp.arange(top)[None, :] + turn) % top, axis=1)


def load_shares(count, total, most, slope, full):
    loads = [(1 << 20) // math.isqrt(grade ** slope) + 1 for grade in range(1, count + 1)]
    largest = most if full else min(most, max(-(-total // count), total * loads[0] // sum(loads)))
    least = 1 if total - largest >= count - 1 else 0
    holding, spare = [largest] + [least] * (count - 1), total - largest - least * (count - 1)
    while spare > 0:
        free = [i for i in range(1, count) if holding[i] < largest] or [i for i in range(1, count) if holding[i] < most]
        whole, remaining = sum([loads[i] for i in free]), spare
        for i in free:
            extra = min(most - holding[i], max(1, remaining * loads[i] // whole), spare)
            holding[i] = holding[i] + extra
            spare = spare - extra
    return np.array(holding)


def normal_values(key, extent, deviation, most, pieces=(), kind=jnp.bfloat16):
    gain = shard_levels(key, extent, pieces, -0.22, 0.18) if pieces else 1.0
    values = jax.random.normal(key, extent, jnp.float32) * deviation * gain
    return jnp.minimum(jnp.maximum(values, -most), most).astype(kind)


def setup_inputs(seed: int = 0) -> dict:
    key_list = jax.random.split(jax.random.key(seed), 17)
    factors = normal_values(key_list[0], (NOCC, NAUX, NVIR), 1.0, 6.0, ((0, 32),), jnp.float32)
    pno_vecs = normal_values(key_list[1], (PAIRS, NVIR, NPNO), (NVIR * 16) ** -0.5, 0.09375, ((0, 32),), jnp.float32)
    pair_occ = draw_pair_occ(jax.random.fold_in(key_list[16], 71), 0)
    pno_count = draw_pno_count(jax.random.fold_in(key_list[16], 71), 0)
    pno_energy = jnp.clip(jnp.exp(math.log(3.0) - 2.3025851 * jax.random.uniform(key_list[4], (PAIRS, NPNO), jnp.float32) ** shard_levels(key_list[4], (PAIRS, NPNO), ((0, 32),), -0.2, 0.2)), 0.3, 3.0)
    occ_energy = jnp.clip(jax.random.uniform(key_list[5], (NOCC,), jnp.float32, -1.5, -0.3), -1.5, -0.3)
    coupi_peer_keys = jax.random.split(jax.random.fold_in(key_list[6], 1), COUPI // COUPI_DEV)
    coupi_peer_turns = jax.random.permutation(jax.random.fold_in(key_list[6], 3), COUPI // COUPI_DEV)
    coupi_peer = jax.vmap(lambda own, number: shared_out(jax.random.fold_in(key_list[6], 2), own, number, COUPI_DEV, N_OCCI, 1, CAPI, 2))(coupi_peer_keys, coupi_peer_turns).reshape((COUPI, 1))
    coupi_slot = with_ends(jax.random.randint(key_list[7], (COUPI,), 0, PAIRS_DEV), jax.random.fold_in(key_list[7], 1), 0, PAIRS_DEV - 1).astype(jnp.int32)
    coupi_target = with_ends(jax.random.randint(key_list[8], (COUPI,), 0, PAIRS_DEV), jax.random.fold_in(key_list[8], 1), 0, PAIRS_DEV - 1).astype(jnp.int32)
    coupi_fock = jnp.clip(jax.random.uniform(key_list[9], (COUPI,), jnp.float32, -0.5, 0.5) * shard_levels(key_list[9], (COUPI,), ((0, 32),), -0.4, 0.0), -0.5, 0.5)
    coupi_correlation = draw_coupi_correlation(jax.random.fold_in(key_list[16], 71), 0)
    coupj_peer_keys = jax.random.split(jax.random.fold_in(key_list[11], 1), COUPJ // COUPJ_DEV)
    coupj_peer_turns = jax.random.permutation(jax.random.fold_in(key_list[11], 3), COUPJ // COUPJ_DEV)
    coupj_peer = jax.vmap(lambda own, number: shared_out(jax.random.fold_in(key_list[11], 2), own, number, COUPJ_DEV, N_OCCJ, 1, CAPJ, 2))(coupj_peer_keys, coupj_peer_turns).reshape((COUPJ, 1))
    coupj_slot = with_ends(jax.random.randint(key_list[12], (COUPJ,), 0, PAIRS_DEV), jax.random.fold_in(key_list[12], 1), 0, PAIRS_DEV - 1).astype(jnp.int32)
    coupj_target = with_ends(jax.random.randint(key_list[13], (COUPJ,), 0, PAIRS_DEV), jax.random.fold_in(key_list[13], 1), 0, PAIRS_DEV - 1).astype(jnp.int32)
    coupj_fock = jnp.clip(jax.random.uniform(key_list[14], (COUPJ,), jnp.float32, -0.5, 0.5) * shard_levels(key_list[14], (COUPJ,), ((0, 32),), -0.4, 0.0), -0.5, 0.5)
    coupj_correlation = draw_coupj_correlation(jax.random.fold_in(key_list[16], 71), 0)
    return {"factors": factors, "pno_vecs": pno_vecs, "pair_occ": pair_occ, "pno_count": pno_count, "pno_energy": pno_energy, "occ_energy": occ_energy, "coupi_peer": coupi_peer, "coupi_slot": coupi_slot, "coupi_target": coupi_target, "coupi_fock": coupi_fock, "coupi_correlation": coupi_correlation, "coupj_peer": coupj_peer, "coupj_slot": coupj_slot, "coupj_target": coupj_target, "coupj_fock": coupj_fock, "coupj_correlation": coupj_correlation}


def coupling_sum(amplitude, correlation, fock, source, target):
    highest = lax.Precision.HIGHEST

    def single(inputs):
        matrix, weight, source_index = inputs
        half_done = jnp.dot(matrix, amplitude[source_index], precision=highest)
        return weight * jnp.dot(half_done, matrix.T, precision=highest)

    coupling_terms = lax.map(single, (correlation, fock, source))
    return jnp.zeros_like(amplitude).at[target].add(coupling_terms)


def reference(factors, pno_vecs, pair_occ, pno_count, pno_energy, occ_energy, coupi_peer, coupi_slot, coupi_target, coupi_fock, coupi_correlation, coupj_peer, coupj_slot, coupj_target, coupj_fock, coupj_correlation):
    highest = lax.Precision.HIGHEST
    pair_count = pair_occ.shape[0]
    occ_first = pair_occ[:, 0]
    occ_second = pair_occ[:, 1]
    groups = pair_count // 8

    def integrals(inputs):
        rows_first, rows_second, vectors = inputs
        left_half = jnp.einsum('gqv,gva->gqa', factors[rows_first], vectors, precision=highest)
        right_half = jnp.einsum('gqv,gva->gqa', factors[rows_second], vectors, precision=highest)
        return jnp.einsum('gqa,gqb->gab', left_half, right_half, precision=highest)

    integral = lax.map(integrals, (occ_first.reshape(groups, 8), occ_second.reshape(groups, 8), pno_vecs.reshape(groups, 8, NVIR, NPNO)))
    integral = integral.reshape(pair_count, NPNO, NPNO)
    live_pno = (jnp.arange(NPNO)[None, :] < pno_count[:, None]).astype(jnp.float32)
    window = live_pno[:, :, None] * live_pno[:, None, :]
    integral = integral * window
    denominator = pno_energy[:, :, None] + pno_energy[:, None, :] - (occ_energy[occ_first] + occ_energy[occ_second])[:, None, None]
    device_i = (jnp.arange(coupi_peer.shape[0]) // COUPI_DEV).astype(jnp.int32)
    target_i = device_i * PAIRS_DEV + coupi_target
    source_i = (coupi_peer[:, 0] * N_OCCJ + device_i % N_OCCJ) * PAIRS_DEV + coupi_slot
    device_j = (jnp.arange(coupj_peer.shape[0]) // COUPJ_DEV).astype(jnp.int32)
    target_j = device_j * PAIRS_DEV + coupj_target
    source_j = ((device_j // N_OCCJ) * N_OCCJ + coupj_peer[:, 0]) * PAIRS_DEV + coupj_slot
    amplitude = -integral / denominator
    residual = jnp.zeros_like(amplitude)
    for iteration in range(ITERS):
        coupled_i = coupling_sum(amplitude, coupi_correlation, coupi_fock, source_i, target_i)
        coupled_j = coupling_sum(amplitude, coupj_correlation, coupj_fock, source_j, target_j)
        residual = window * (integral + denominator * amplitude - coupled_i - coupled_j)
        amplitude = amplitude - residual / denominator
    return amplitude, residual
```

```python
import functools

import jax
import jax.numpy as jnp
from jax import lax
from jax.experimental import pallas as pl
from jax.experimental.pallas import tpu as pltpu
from jax.sharding import PartitionSpec as P


BATCH = 4
CHUNK = 8
VMEM_BYTES = 56 << 20
ANY = pl.BlockSpec(memory_space=pl.ANY)
SMEM = pl.BlockSpec(memory_space=pltpu.SMEM)
VMEM = pl.BlockSpec(memory_space=pltpu.VMEM)
F32 = jnp.float32
BF16 = jnp.bfloat16


def split(x):
    lead = x.astype(BF16)
    return lead, (x - lead.astype(F32)).astype(BF16)


def wide_left(x):
    lead, rest = split(x)
    return jnp.concatenate([lead, lead, rest], axis=1)


def wide_right(x, axis):
    lead, rest = split(x)
    return jnp.concatenate([lead, rest, lead], axis=axis)


def dot_nn(left, right):
    return lax.dot_general(left, right, (((1,), (0,)), ((), ())), preferred_element_type=F32)


def dot_nt(left, right):
    return lax.dot_general(left, right, (((1,), (1,)), ((), ())), preferred_element_type=F32)


def pair_window(count, width):
    row = lax.broadcasted_iota(jnp.int32, (width, width), 0)
    column = lax.broadcasted_iota(jnp.int32, (width, width), 1)
    return (row < count) & (column < count)


def pair_denominator(energy_ref, p, occ_sum, width):
    energies = jnp.broadcast_to(energy_ref[pl.ds(p, 1), :], (width, width))
    return energies + energies.T - occ_sum


def each_send(sizes, incoming, me, rows_ref, sends, sems, act):
    for k, send in enumerate(sends):
        cap = sizes[1]
        peer = me ^ k

        def one(r, carry, k=k, send=send, peer=peer, cap=cap):
            row = incoming[peer * cap + r]

            @pl.when(row >= 0)
            def _():
                copy = pltpu.make_async_copy(rows_ref.at[jnp.maximum(row, 0)], send.at[r], sems.at[k, r])
                act(copy)

            return carry

        lax.fori_loop(0, cap, one, 0)


def integral_kernel(
    *refs, blocks, columns, owned, last, sizes_i, sizes_j
):
    refs = list(refs)
    take = lambda n: [refs.pop(0) for _ in range(n)]
    order, bounds, row_of, col_of, count, occ_sum = take(6)
    me, incoming_i, incoming_j = take(3) if last else (None, None, None)
    energy, vectors = take(2)
    row_blocks, col_blocks = take(blocks), take(columns)
    if bounds.shape[0] and last is not None:
        old_amp, old_base = take(2)
    else:
        old_amp = old_base = None
    amp_out, base_out = take(2)
    if last:
        sends_i, sends_j = take(sizes_i[0]), take(sizes_j[0])
    qbuf, abuf, bbuf, rbuf, cbuf, ccat, lead, rest = take(8)
    qsem, asem, bsem, rsem, csem = take(5)
    if last:
        sisem, sjsem = take(2)
    width = abuf.shape[1]
    virs = rbuf.shape[2]
    start, stop = bounds[0], bounds[1]

    for b in range(blocks):
        pltpu.make_async_copy(row_blocks[b], rbuf.at[pl.ds(b * owned, owned)], rsem.at[b]).start()
    for b in range(columns):
        pltpu.make_async_copy(col_blocks[b], cbuf.at[pl.ds(b * owned, owned)], csem.at[b]).start()

    def load(t, carry):
        pltpu.make_async_copy(vectors.at[order[t]], qbuf.at[t], qsem.at[t]).start()
        return carry

    lax.fori_loop(start, stop, load, 0)
    if last:

        def load_old(t, carry):
            p = order[t]
            pltpu.make_async_copy(old_amp.at[p], abuf.at[p], asem.at[t]).start()
            return carry

        lax.fori_loop(0, start, load_old, 0)

    for b in range(columns):
        pltpu.make_async_copy(col_blocks[b], cbuf.at[pl.ds(b * owned, owned)], csem.at[b]).wait()
    for b in range(blocks):
        pltpu.make_async_copy(row_blocks[b], rbuf.at[pl.ds(b * owned, owned)], rsem.at[b]).wait()

    ncol = columns * owned
    nrow = blocks * owned

    def prepare(c, carry):
        ccat[c] = wide_right(cbuf[c], 0)
        return carry

    lax.fori_loop(0, ncol, prepare, 0)

    def gram(b, carry):
        left = wide_left(rbuf[b].T)

        def column(c, inner):
            product = dot_nn(left, ccat[c])
            top, low = split(product)
            lead[b * ncol + c] = top
            rest[b * ncol + c] = low
            return inner

        return lax.fori_loop(0, ncol, column, carry)

    lax.fori_loop(0, nrow, gram, 0)

    def batch(g, carry):
        first = start + g * BATCH
        places = [jnp.minimum(first + j, stop - 1) for j in range(BATCH)]
        for j in range(BATCH):

            @pl.when(first + j < stop)
            def _(j=j):
                pltpu.make_async_copy(vectors.at[0], qbuf.at[first + j], qsem.at[first + j]).wait()

        results = []
        for j in range(BATCH):
            p = order[places[j]]
            q = qbuf[places[j]]
            cell = row_of[p] * ncol + col_of[p]
            top, low = lead[cell], rest[cell]
            half = dot_nn(wide_left(q.T), jnp.concatenate([top, low, top], axis=0))
            integral = dot_nn(wide_left(half), wide_right(q, 0))
            results.append((p, integral))
        for j in range(BATCH):
            p, integral = results[j]
            integral = jnp.where(pair_window(count[p], width), integral, 0.0)
            denominator = pair_denominator(energy, p, occ_sum[p], width)
            amplitude = -integral / denominator
            abuf[p] = amplitude
            bbuf[p] = integral + denominator * amplitude
        for j in range(BATCH):

            @pl.when(first + j < stop)
            def _(j=j):
                p = order[places[j]]
                pltpu.make_async_copy(abuf.at[p], amp_out.at[p], asem.at[first + j]).start()
                pltpu.make_async_copy(bbuf.at[p], base_out.at[p], bsem.at[first + j]).start()

        return carry

    if last:

        def wait_old(t, carry):
            pltpu.make_async_copy(old_amp.at[0], abuf.at[0], asem.at[t]).wait()
            return carry

        lax.fori_loop(0, start, wait_old, 0)
    lax.fori_loop(0, (stop - start + BATCH - 1) // BATCH, batch, 0)
    if last:
        here_i, here_j = me[0], me[1]
        begin = lambda copy: copy.start()
        finish = lambda copy: copy.wait()
        each_send(sizes_i, incoming_i, here_i, abuf, sends_i, sisem, begin)
        each_send(sizes_j, incoming_j, here_j, abuf, sends_j, sjsem, begin)

    def wait_out(t, carry):
        p = order[t]
        pltpu.make_async_copy(abuf.at[p], amp_out.at[p], asem.at[t]).wait()
        pltpu.make_async_copy(bbuf.at[p], base_out.at[p], bsem.at[t]).wait()
        return carry

    lax.fori_loop(start, stop, wait_out, 0)
    if last:
        each_send(sizes_i, incoming_i, here_i, abuf, sends_i, sisem, finish)
        each_send(sizes_j, incoming_j, here_j, abuf, sends_j, sjsem, finish)


def couplings(sources, counts, first, order, target, fock, correlation, xbuf, cbuf, xsem, csem, slots):
    total = order.shape[0]
    at = first
    ends = []
    for k, source in sources:
        number = counts[k]

        def one(r, carry, source=source, at=at):
            e = at - first + r
            pltpu.make_async_copy(source.at[r], xbuf.at[e], xsem.at[e]).start()
            return carry

        lax.fori_loop(0, number, one, 0)
        at = at + number
    used = at - first
    groups = (used + CHUNK - 1) // CHUNK

    def load(e, carry):
        c = order[jnp.minimum(first + e, total - 1)]
        pltpu.make_async_copy(correlation.at[c], cbuf.at[e], csem.at[e]).start()

        @pl.when(e >= used)
        def _():
            xbuf[e] = jnp.zeros(xbuf.shape[1:], F32)

        return carry

    lax.fori_loop(0, groups * CHUNK, load, 0)

    def add(acc):
        def chunk(g, carry):
            for j in range(CHUNK):
                e = g * CHUNK + j
                pltpu.make_async_copy(correlation.at[0], cbuf.at[e], csem.at[e]).wait()

                @pl.when(e < used)
                def _(e=e):
                    pltpu.make_async_copy(correlation.at[0], xbuf.at[e], xsem.at[e]).wait()

            terms = []
            for j in range(CHUNK):
                e = g * CHUNK + j
                matrix = cbuf[e]
                top, low = split(matrix)
                half = dot_nn(jnp.concatenate([top, top, low], axis=1), wide_right(xbuf[e], 0))
                terms.append(dot_nt(wide_left(half), jnp.concatenate([top, low, top], axis=1)))
            for j in range(CHUNK):
                e = g * CHUNK + j
                c = order[jnp.minimum(first + e, total - 1)]
                weight = jnp.where(e < used, fock[c], 0.0)
                t = target[c]
                acc[t] += weight * terms[j]
            return carry

        lax.fori_loop(0, groups, chunk, 0)

    return add


def first_kernel(*refs, peers_i, peers_j, second):
    refs = list(refs)
    take = lambda n: [refs.pop(0) for _ in range(n)]
    order_i, counts_i, target_i, fock_i, order_j, counts_j, target_j, fock_j = take(8)
    if second:
        occ_sum, energy = take(2)
    own_j, = take(1)
    sources_i = take(peers_i)
    corr_i, corr_j, start_in = take(3)
    if second:
        amp_in, = take(1)
    partial, = take(1)
    if second:
        amp_out, = take(1)
    acc, xbuf, cbuf, ybuf, dbuf = take(5)
    if second:
        abuf, = take(1)
    sem, xsem, csem, ysem, dsem = take(5)
    pairs, width = acc.shape[0], acc.shape[1]
    pltpu.make_async_copy(start_in, acc, sem.at[0]).start()
    if second:
        pltpu.make_async_copy(amp_in, abuf, sem.at[1]).start()
    add_i = couplings(
        [(k, sources_i[k]) for k in range(1, peers_i)] + [(0, sources_i[0])],
        counts_i, 0, order_i, target_i, fock_i, corr_i, xbuf, cbuf, xsem, csem, None)
    total = order_j.shape[0]
    add_j = couplings(
        [(0, own_j)], counts_j, total - counts_j[0], order_j, target_j, fock_j, corr_j, ybuf, dbuf, ysem, dsem, None)
    pltpu.make_async_copy(start_in, acc, sem.at[0]).wait()
    if second:
        pltpu.make_async_copy(amp_in, abuf, sem.at[1]).wait()

        def settle(p, carry):
            residual = acc[p]
            denominator = pair_denominator(energy, p, occ_sum[p], width)
            step = residual / denominator
            abuf[p] = abuf[p] - step
            acc[p] = residual - denominator * step
            return carry

        lax.fori_loop(0, pairs, settle, 0)
        pltpu.make_async_copy(abuf, amp_out, sem.at[1]).start()
    add_i(acc)
    add_j(acc)
    pltpu.make_async_copy(acc, partial, sem.at[0]).start()
    pltpu.make_async_copy(acc, partial, sem.at[0]).wait()
    if second:
        pltpu.make_async_copy(abuf, amp_out, sem.at[1]).wait()


def second_kernel(*refs, peers_i, peers_j, sizes_i, sizes_j, second):
    refs = list(refs)
    take = lambda n: [refs.pop(0) for _ in range(n)]
    order_j, counts_j, target_j, fock_j, count, occ_sum = take(6)
    if not second:
        me, incoming_i, incoming_j = take(3)
    energy, = take(1)
    sources_j = take(peers_j - 1)
    corr_j, partial = take(2)
    if second:
        amp_in, = take(1)
    residual_out, = take(1)
    if second:
        amp_out, = take(1)
    else:
        sends_i, sends_j = take(peers_i), take(peers_j)
    acc, ebuf, xbuf, cbuf = take(4)
    sem, xsem, csem, osem, psem = take(5)
    if not second:
        sisem, sjsem = take(2)
    pairs, width = acc.shape[0], acc.shape[1]
    pltpu.make_async_copy(partial, acc, sem.at[0]).start()
    if second:
        pltpu.make_async_copy(amp_in, ebuf, sem.at[1]).start()
    add_j = couplings(
        [(k, sources_j[k - 1]) for k in range(1, peers_j)],
        counts_j, 0, order_j, target_j, fock_j, corr_j, xbuf, cbuf, xsem, csem, None)
    pltpu.make_async_copy(partial, acc, sem.at[0]).wait()
    add_j(acc)
    if second:
        pltpu.make_async_copy(amp_in, ebuf, sem.at[1]).wait()

    def settle(p, carry):
        residual = jnp.where(pair_window(count[p], width), acc[p], 0.0)
        acc[p] = residual
        step = residual / pair_denominator(energy, p, occ_sum[p], width)
        ebuf[p] = ebuf[p] - step if second else step
        pltpu.make_async_copy(acc.at[p], residual_out.at[p], osem.at[p]).start()
        if second:
            pltpu.make_async_copy(ebuf.at[p], amp_out.at[p], psem.at[p]).start()
        return carry

    lax.fori_loop(0, pairs, settle, 0)
    if not second:
        here_i, here_j = me[0], me[1]
        begin = lambda copy: copy.start()
        finish = lambda copy: copy.wait()
        each_send(sizes_i, incoming_i, here_i, ebuf, sends_i, sisem, begin)
        each_send(sizes_j, incoming_j, here_j, ebuf, sends_j, sjsem, begin)
        each_send(sizes_i, incoming_i, here_i, ebuf, sends_i, sisem, finish)
        each_send(sizes_j, incoming_j, here_j, ebuf, sends_j, sjsem, finish)

    def wait_out(p, carry):
        pltpu.make_async_copy(acc.at[p], residual_out.at[p], osem.at[p]).wait()
        if second:
            pltpu.make_async_copy(ebuf.at[p], amp_out.at[p], psem.at[p]).wait()
        return carry

    lax.fori_loop(0, pairs, wait_out, 0)


def call(kernel, outs, specs, scratch, args, flops, moved, aliases=None):
    return pl.pallas_call(
        kernel,
        out_shape=outs,
        in_specs=specs,
        out_specs=[ANY] * len(outs),
        scratch_shapes=scratch,
        input_output_aliases=aliases or {},
        compiler_params=pltpu.CompilerParams(vmem_limit_bytes=VMEM_BYTES),
        cost_estimate=pl.CostEstimate(flops=flops, bytes_accessed=moved, transcendentals=0),
    )(*args)


def exchange(x, axis, k):
    size = lax.axis_size(axis)
    return lax.ppermute(x, axis, [(s, s ^ k) for s in range(size)])


def spread(own, axis):
    blocks = {0: own}
    bit = lax.axis_size(axis) // 2
    while bit:
        for k in list(blocks):
            blocks[k | bit] = exchange(blocks[k], axis, bit)
        bit //= 2
    return [blocks[k] for k in range(lax.axis_size(axis))]


def sort_order(key):
    number = key.shape[0]
    at = jnp.arange(number)
    ahead = (key[None, :] < key[:, None]) | ((key[None, :] == key[:, None]) & (at[None, :] < at[:, None]))
    rank = jnp.sum(ahead.astype(jnp.int32), axis=1)
    return jnp.sum(jnp.where(rank[:, None] == at[None, :], at[:, None], 0), axis=0).astype(jnp.int32)


def arrange(peer, slot, me, size):
    number = peer.shape[0]
    cap = max(2, 2 * number // size)
    member = (peer[:, None] == jnp.arange(size)[None, :]).astype(jnp.int32)
    before = jnp.sum((jnp.cumsum(member, axis=0) - member) * member, axis=1)
    position = peer * cap + before
    matches = position[:, None] == jnp.arange(size * cap)[None, :]
    requests = jnp.sum(jnp.where(matches, slot[:, None] + 1, 0), axis=0) - 1
    shift = peer ^ me
    order = sort_order(jnp.where(shift == 0, size, shift))
    counts = jnp.sum((shift[:, None] == jnp.arange(size)[None, :]).astype(jnp.int32), axis=0)
    return requests.reshape(size, cap).astype(jnp.int32), order, counts.astype(jnp.int32), cap


def local(
    factors,
    pno_vecs,
    pair_occ,
    pno_count,
    pno_energy,
    occ_energy,
    coupi_peer,
    coupi_slot,
    coupi_target,
    coupi_fock,
    coupi_correlation,
    coupj_peer,
    coupj_slot,
    coupj_target,
    coupj_fock,
    coupj_correlation,
):
    size_i, size_j = lax.axis_size("occi"), lax.axis_size("occj")
    me_i, me_j = lax.axis_index("occi"), lax.axis_index("occj")
    owned, aux, virs = factors.shape
    pairs, _, width = pno_vecs.shape
    dma = pltpu.SemaphoreType.DMA

    rows = spread(factors, "occj")
    columns = spread(factors, "occi")

    req_i, order_i, counts_i, cap_i = arrange(coupi_peer[:, 0], coupi_slot, me_i, size_i)
    req_j, order_j, counts_j, cap_j = arrange(coupj_peer[:, 0], coupj_slot, me_j, size_j)
    incoming_i = lax.all_to_all(req_i, "occi", split_axis=0, concat_axis=0, tiled=True).reshape(-1)
    incoming_j = lax.all_to_all(req_j, "occj", split_axis=0, concat_axis=0, tiled=True).reshape(-1)
    sizes_i, sizes_j = (size_i, cap_i), (size_j, cap_j)
    me = jnp.stack([me_i, me_j]).astype(jnp.int32)

    first = pair_occ[:, 0] - me_i * owned * size_j
    shift_j = (first // owned) ^ me_j
    second = pair_occ[:, 1]
    shift_i = (second // owned // size_j) ^ me_i
    col_of = (shift_i * owned + second % owned).astype(jnp.int32)
    occ_sum = occ_energy[pair_occ[:, 0]] + occ_energy[pair_occ[:, 1]]
    order = sort_order(shift_j)

    pair_shape = jax.ShapeDtypeStruct((pairs, width, width), F32)
    pair_buf = pltpu.VMEM((pairs, width, width), F32)
    sends = [jax.ShapeDtypeStruct((cap_i, width, width), F32)] * size_i
    sends += [jax.ShapeDtypeStruct((cap_j, width, width), F32)] * size_j
    send_sems = [dma((size_i, cap_i)), dma((size_j, cap_j))]
    pair_bytes = 4 * pairs * width * width

    cuts = [0, size_j // 2, size_j * 3 // 4, size_j]
    amplitude = base = None
    for g in range(len(cuts) - 1):
        low, high = cuts[g], cuts[g + 1]
        last = g == len(cuts) - 2
        blocks = high - low
        bounds = jnp.stack([jnp.sum(shift_j < low), jnp.sum(shift_j < high)]).astype(jnp.int32)
        row_of = ((shift_j - low) * owned + first % owned).astype(jnp.int32)
        args = [order, bounds, row_of, col_of, pno_count, occ_sum]
        specs = [SMEM] * 6
        if last:
            args += [me, incoming_i, incoming_j]
            specs += [SMEM] * 3
        args += [pno_energy, pno_vecs]
        specs += [VMEM, ANY]
        args += rows[low:high] + columns
        specs += [ANY] * (blocks + size_i)
        aliases = {}
        if g:
            aliases = {len(args): 0, len(args) + 1: 1}
            args += [amplitude, base]
            specs += [ANY, ANY]
        scratch = [
            pltpu.VMEM((pairs, virs, width), F32),
            pair_buf,
            pair_buf,
            pltpu.VMEM((blocks * owned, aux, virs), F32),
            pltpu.VMEM((size_i * owned, aux, virs), F32),
            pltpu.VMEM((size_i * owned, 3 * aux, virs), BF16),
            pltpu.VMEM((blocks * size_i * owned * owned, virs, virs), BF16),
            pltpu.VMEM((blocks * size_i * owned * owned, virs, virs), BF16),
            dma((pairs,)),
            dma((pairs,)),
            dma((pairs,)),
            dma((blocks,)),
            dma((size_i,)),
        ]
        outs = [pair_shape, pair_shape]
        if last:
            outs += sends
            scratch += send_sems
        kernel = functools.partial(
            integral_kernel,
            blocks=blocks,
            columns=size_i,
            owned=owned,
            last=last if g else None,
            sizes_i=sizes_i,
            sizes_j=sizes_j,
        )
        share = blocks / size_j
        results = call(
            kernel, outs, specs, scratch, args,
            int(share * 6 * virs * (2 * size_j * size_i * aux * virs + pairs * 2 * width * (virs + width))),
            int(share * 4 * pairs * width * (virs + 2 * width) + 4 * (blocks + size_i) * aux * virs),
            aliases)
        amplitude, base = results[:2]
    sent = results[2:]

    start, residual = base, None
    for iteration in range(2):
        again = iteration == 1
        sent_i, sent_j = sent[:size_i], sent[size_i:]
        got_j = [exchange(sent_j[k], "occj", k) for k in reversed(range(1, size_j))][::-1]
        got_i = [sent_i[0]] + [exchange(sent_i[k], "occi", k) for k in range(1, size_i)]
        sign = 1.0 if again else -1.0
        fock_i, fock_j = sign * coupi_fock, sign * coupj_fock
        number_i, number_j = coupi_slot.shape[0], coupj_slot.shape[0]
        tables_i = [order_i, counts_i, coupi_target, fock_i]
        tables_j = [order_j, counts_j, coupj_target, fock_j]
        args = tables_i + tables_j
        specs = [SMEM] * 8
        if again:
            args += [occ_sum, pno_energy]
            specs += [SMEM, VMEM]
        args += [sent_j[0]] + got_i + [coupi_correlation, coupj_correlation, start]
        specs += [ANY] * (4 + size_i)
        if again:
            args += [amplitude]
            specs += [ANY]
        up = lambda n: (n + CHUNK - 1) // CHUNK * CHUNK
        matrix = lambda n: pltpu.VMEM((up(n), width, width), F32)
        scratch = [pair_buf, matrix(number_i), matrix(number_i), matrix(cap_j), matrix(cap_j)]
        if again:
            scratch += [pair_buf]
        scratch += [dma((2,)), dma((up(number_i),)), dma((up(number_i),)), dma((up(cap_j),)), dma((up(cap_j),))]
        results = call(
            functools.partial(first_kernel, peers_i=size_i, peers_j=size_j, second=again),
            [pair_shape] * (2 if again else 1), specs, scratch, args,
            12 * number_i * width**3, 2 * pair_bytes + 8 * number_i * width * width)
        partial = results[0]
        if again:
            amplitude = results[1]
        args = tables_j + [pno_count, occ_sum]
        specs = [SMEM] * 6
        if not again:
            args += [me, incoming_i, incoming_j]
            specs += [SMEM] * 3
        args += [pno_energy] + got_j + [coupj_correlation, partial]
        specs += [VMEM] + [ANY] * (size_j + 1)
        outs = [pair_shape]
        if again:
            args += [amplitude]
            specs += [ANY]
            outs += [pair_shape]
        else:
            outs += sends
        scratch = [pair_buf, pair_buf, matrix(number_j), matrix(number_j)]
        scratch += [dma((2,)), dma((up(number_j),)), dma((up(number_j),)), dma((pairs,)), dma((pairs,))]
        if not again:
            scratch += send_sems
        results = call(
            functools.partial(
                second_kernel, peers_i=size_i, peers_j=size_j, sizes_i=sizes_i, sizes_j=sizes_j, second=again),
            outs, specs, scratch, args,
            12 * number_j * width**3, 3 * pair_bytes + 8 * number_j * width * width)
        residual = results[0]
        if again:
            amplitude = results[1]
        else:
            start, sent = residual, results[1:]
    return amplitude, residual


def solution(mesh):
    lead = ("occi", "occj")
    placed = (
        P(lead, None, None),
        P(lead, None, None),
        P(lead, None),
        P(lead),
        P(lead, None),
        P(),
        P(lead, None),
        P(lead),
        P(lead),
        P(lead),
        P(lead, None, None),
        P(lead, None),
        P(lead),
        P(lead),
        P(lead),
        P(lead, None, None),
    )
    return jax.shard_map(
        local,
        mesh=mesh,
        in_specs=placed,
        out_specs=(P(lead, None, None), P(lead, None, None)),
        check_vma=False,
    )
```

```python
import functools
import math

import jax
import jax.numpy as jnp
from jax import lax
from jax.experimental import pallas as pl
from jax.experimental.pallas import tpu as pltpu
from jax.sharding import PartitionSpec as P


BATCH = 8
CHUNK = 4
SETTLE = 4
FLAGS = {}
ANY = pl.BlockSpec(memory_space=pl.ANY)
SMEM = pl.BlockSpec(memory_space=pltpu.SMEM)
VMEM = pl.BlockSpec(memory_space=pltpu.VMEM)
HBM = pl.BlockSpec(memory_space=pltpu.HBM)
F32 = jnp.float32
BF16 = jnp.bfloat16


def split(x):
    lead = x.astype(BF16)
    return lead, (x - lead.astype(F32)).astype(BF16)


def wide_left(x):
    lead, rest = split(x)
    return jnp.concatenate([lead, lead, rest], axis=1)


def wide_right(x, axis):
    lead, rest = split(x)
    return jnp.concatenate([lead, rest, lead], axis=axis)


def dot_nn(left, right):
    return lax.dot_general(left, right, (((1,), (0,)), ((), ())), preferred_element_type=F32)


def dot_nt(left, right):
    return lax.dot_general(left, right, (((1,), (1,)), ((), ())), preferred_element_type=F32)


def pair_window(count, width):
    row = lax.broadcasted_iota(jnp.int32, (width, width), 0)
    column = lax.broadcasted_iota(jnp.int32, (width, width), 1)
    return (row < count) & (column < count)


def pair_denominator(energy_ref, p, occ_sum, width):
    energies = jnp.broadcast_to(energy_ref[pl.ds(p, 1), :], (width, width))
    return energies + energies.T - occ_sum


def index_kernel(
    *refs, at, owned, rank_i, rank_j
):
    inputs, (table, weights), local, sem = refs[:10], refs[10:12], refs[12:22], refs[22]
    copies = [pltpu.make_async_copy(inputs[n], local[n], sem.at[n]) for n in range(10)]
    for copy in copies:
        copy.start()
    for copy in copies:
        copy.wait()
    first, second, count, peer_i, target_i, fock_i, peer_j, target_j, fock_j, energy = local
    me_i, me_j = lax.axis_index("occi"), lax.axis_index("occj")
    size_i, size_j = len(rank_i), len(rank_j)
    table[at["me"]] = me_i
    table[at["me"] + 1] = me_j
    pairs = first.shape[0]

    def sort(number, size, rank, key, start, counts, cursor, place):
        for k in range(size):
            table[counts + k] = 0

        def tally(c, carry):
            table[counts + key(c)] += 1
            return carry

        lax.fori_loop(0, number, tally, 0)
        total = 0
        for k in sorted(range(size), key=lambda k: rank[k]):
            table[start + k] = total
            table[cursor + k] = total
            total = total + table[counts + k]

        def settle(c, carry):
            k = key(c)
            e = table[cursor + k]
            table[cursor + k] = e + 1
            place(c, k, e)
            return carry

        lax.fori_loop(0, number, settle, 0)

    def place_pair(p, k, e):
        table[at["order"] + e] = p

    def shift_of_pair(p):
        return ((first[p] - me_i * (owned * size_j)) // owned) ^ me_j

    sort(pairs, size_j, list(range(size_j)), shift_of_pair, at["start"], at["counts"], at["cursor"], place_pair)

    def describe(p, carry):
        one, two = first[p], second[p]
        table[at["row"] + p] = shift_of_pair(p) * owned + one % owned
        table[at["col"] + p] = ((two // owned // size_j) ^ me_i) * owned + two % owned
        weights[at["occ"] + p] = energy[one] + energy[two]
        table[at["count"] + p] = count[p]
        return carry

    lax.fori_loop(0, pairs, describe, 0)

    def one_list(name, peer, target, fock, me, size, rank):
        def place(c, k, e):
            table[at["order_" + name] + e] = c
            table[at["target_" + name] + e] = target[c]
            weights[at["fock_" + name] + e] = fock[c]

        sort(peer.shape[0], size, rank, lambda c: peer[c] ^ me, at["start_" + name], at["counts_" + name],
             at["cursor_" + name], place)

    one_list("i", peer_i, target_i, fock_i, me_i, size_i, rank_i)
    one_list("j", peer_j, target_j, fock_j, me_j, size_j, rank_j)


def read_requests(peer_ref, slot_ref, mine, caps, requests):
    lists, lanes = requests.shape
    lane = lax.broadcasted_iota(jnp.int32, (lists, lanes), 1)
    match = peer_ref[...] == mine
    ones = match.astype(F32)
    ahead = lax.broadcasted_iota(jnp.int32, (lanes, lanes), 0) < lax.broadcasted_iota(jnp.int32, (lanes, lanes), 1)
    place = dot_nn(ones.astype(BF16), ahead.astype(F32).astype(BF16))
    rows = jnp.where(lane == 127, jnp.sum(ones, axis=1, keepdims=True), 0.0)
    for r in range(caps):
        here = jnp.where(match & (place == r), slot_ref[...], 0.0)
        rows = jnp.where(lane == r, jnp.sum(here, axis=1, keepdims=True), rows)
    requests[...] = rows.astype(jnp.int32)


def fill_sends(cap, incoming, first, rows_ref, sends):
    step = math.gcd(cap, 4)
    for k, send in enumerate(sends):
        n = first + k

        def some(g, carry, send=send, n=n):
            for j in range(step):
                send[g * step + j] = rows_ref[incoming[n, g * step + j]]
            return carry

        lax.fori_loop(0, jnp.minimum((incoming[n, 127] + step - 1) // step, cap // step), some, 0)


def integral_kernel(*refs, at, low, high, columns, owned, aux, first, last, sizes_i, sizes_j):
    refs = list(refs)
    take = lambda n: [refs.pop(0) for _ in range(n)]
    blocks = high - low
    table, weights = take(2)
    energy_in, vectors = take(2)
    row_blocks, col_blocks = take(blocks), take(columns)
    if last:
        others = take(low)
    if not first:
        old_amp, _ = take(2)
    amp_out, base_out = take(2)
    if last:
        (incoming,) = take(1)
        sends_i, sends_j = take(sizes_i[0]), take(sizes_j[0])
    amp, base, qbuf, energy, ccat, lead, rest, qsem, esem, asem, bsem = take(11)
    if last:
        peer_buf, slot_buf, requests, rsem = take(4)
    pairs, width = amp.shape[0], amp.shape[1]
    start = table[at["start"] + low]
    stop = table[at["start"] + high] if high < sizes_j[0] else pairs
    pltpu.make_async_copy(energy_in, energy, esem.at[0]).start()

    def load(t, carry):
        pltpu.make_async_copy(vectors.at[table[at["order"] + t]], qbuf.at[t], qsem.at[t]).start()
        return carry

    lax.fori_loop(start, stop, load, 0)
    if last:

        def load_old(t, carry):
            p = table[at["order"] + t]
            pltpu.make_async_copy(old_amp.at[p], amp.at[p], asem.at[t]).start()
            return carry

        lax.fori_loop(0, start, load_old, 0)
        sources = [(block, 2) for block in others + row_blocks] + [(block, 0) for block in col_blocks]
        peer_buf[...] = jnp.full(peer_buf.shape, -1.0, F32)
        slot_buf[...] = jnp.zeros(slot_buf.shape, F32)
        for n, (block, row) in enumerate(sources):
            peer_buf[n : n + 1] = block[0, aux + row : aux + row + 1, :128]
            slot_buf[n : n + 1] = block[0, aux + row + 1 : aux + row + 2, :128]
        along_j = lax.broadcasted_iota(jnp.int32, peer_buf.shape, 0) < sizes_j[0]
        mine = jnp.where(along_j, table[at["me"] + 1], table[at["me"]]).astype(F32)
        read_requests(peer_buf, slot_buf, mine, max(sizes_i[1], sizes_j[1]), requests)
        tell = pltpu.make_async_copy(requests, incoming, rsem.at[0])
        tell.start()
    order = lambda t: table[at["order"] + t]
    ncol = columns * owned
    for b in range(columns):
        for o in range(owned):
            ccat[b * owned + o] = wide_right(col_blocks[b][o, :aux], 0)
    for b in range(blocks):
        for o in range(owned):
            left = wide_left(row_blocks[b][o, :aux].T)

            def column(c, inner, left=left, cell=(b * owned + o) * ncol):
                top, rem = split(dot_nn(left, ccat[c]))
                lead[cell + c] = top
                rest[cell + c] = rem
                return inner

            lax.fori_loop(0, ncol, column, 0)

    pltpu.make_async_copy(energy_in, energy, esem.at[0]).wait()

    def batch(g, carry):
        head = start + g * BATCH
        for j in range(BATCH):

            @pl.when(head + j < stop)
            def _(j=j):
                pltpu.make_async_copy(vectors.at[0], qbuf.at[head + j], qsem.at[head + j]).wait()

        results = []
        for j in range(BATCH):
            t = jnp.minimum(head + j, stop - 1)
            p = order(t)
            q = qbuf[t]
            cell = (table[at["row"] + p] - low * owned) * ncol + table[at["col"] + p]
            top, rem = lead[cell], rest[cell]
            half = dot_nn(wide_left(q.T), jnp.concatenate([top, rem, top], axis=0))
            integral = dot_nn(wide_left(half), wide_right(q, 0))
            results.append((p, integral))
        for j in range(BATCH):
            p, integral = results[j]
            integral = jnp.where(pair_window(table[at["count"] + p], width), integral, 0.0)
            denominator = pair_denominator(energy, p, weights[at["occ"] + p], width)
            amplitude = -integral / denominator
            amp[p] = amplitude
            base[p] = integral + denominator * amplitude
        for j in range(BATCH):

            @pl.when(head + j < stop)
            def _(j=j):
                p = order(head + j)
                pltpu.make_async_copy(amp.at[p], amp_out.at[p], asem.at[head + j]).start()
                pltpu.make_async_copy(base.at[p], base_out.at[p], bsem.at[head + j]).start()

        return carry

    lax.fori_loop(0, (stop - start + BATCH - 1) // BATCH, batch, 0)
    if last:

        def wait_old(t, carry):
            pltpu.make_async_copy(old_amp.at[0], amp.at[0], asem.at[t]).wait()
            return carry

        lax.fori_loop(0, start, wait_old, 0)
        tell.wait()
        fill_sends(sizes_j[1], incoming, 0, amp, sends_j)
        fill_sends(sizes_i[1], incoming, sizes_j[0], amp, sends_i)

    def wait_out(t, carry):
        p = order(t)
        pltpu.make_async_copy(amp.at[p], amp_out.at[p], asem.at[t]).wait()
        pltpu.make_async_copy(base.at[p], base_out.at[p], bsem.at[t]).wait()
        return carry

    lax.fori_loop(start, stop, wait_out, 0)


def add_couplings(table, weights, at, name, sign, shifts, sources, number, correlation, xbuf, acc):
    first = table[at["start_" + name] + shifts[0]]
    used = 0
    for k, source in zip(shifts, sources):
        here = table[at["counts_" + name] + k]

        def one(r, carry, source=source, base=used):
            xbuf[base + r] = source[r]
            return carry

        lax.fori_loop(0, here, one, 0)
        used = used + here
    groups = (used + CHUNK - 1) // CHUNK

    def clear(e, carry):
        xbuf[e] = jnp.zeros(xbuf.shape[1:], F32)
        return carry

    lax.fori_loop(used, groups * CHUNK, clear, 0)

    def chunk(g, carry):
        terms = []
        for j in range(CHUNK):
            e = g * CHUNK + j
            matrix = correlation[table[at["order_" + name] + jnp.minimum(first + e, number - 1)]]
            top, low = split(matrix)
            half = dot_nn(jnp.concatenate([top, top, low], axis=1), wide_right(xbuf[e], 0))
            terms.append(dot_nt(wide_left(half), jnp.concatenate([top, low, top], axis=1)))
        for j in range(CHUNK):
            e = g * CHUNK + j
            s = jnp.minimum(first + e, number - 1)
            weight = jnp.where(e < used, sign * weights[at["fock_" + name] + s], 0.0)
            acc[table[at["target_" + name] + s]] += weight * terms[j]
        return carry

    lax.fori_loop(0, groups, chunk, 0)


def grouped(number, step):
    size = math.gcd(number, SETTLE)

    def some(g, carry):
        step([g * size + j for j in range(size)])
        return carry

    lax.fori_loop(0, number // size, some, 0)


def near_kernel(*refs, at, sign, shifts_i, number_i, number_j, second):
    refs = list(refs)
    take = lambda n: [refs.pop(0) for _ in range(n)]
    table, weights = take(2)
    (energy,) = take(1)
    (own_j,) = take(1)
    sources_i = take(len(shifts_i))
    corr_i, corr_j = take(2)
    start_in, = take(1)
    if second:
        amp_in, acc, amp, xbuf, sem = take(5)
    else:
        acc, xbuf, sem = take(3)
    pairs, width = acc.shape[0], acc.shape[1]
    fetch = pltpu.make_async_copy(amp_in if second else start_in, amp if second else acc, sem.at[0])
    fetch.start()
    fetch.wait()
    if second:

        def settle(group):
            for p in group:
                residual = start_in[p]
                denominator = pair_denominator(energy, p, weights[at["occ"] + p], width)
                step = residual / denominator
                amp[p] = amp[p] - step
                acc[p] = residual - denominator * step

        grouped(pairs, settle)
    add_couplings(table, weights, at, "i", sign, shifts_i, sources_i, number_i, corr_i, xbuf, acc)
    add_couplings(table, weights, at, "j", sign, [0], [own_j], number_j, corr_j, xbuf, acc)


def carry_over(source, acc):
    def some(group):
        for p in group:
            acc[p] = source[p]

    grouped(acc.shape[0], some)


def middle_kernel(*refs, at, sign, shifts, number):
    refs = list(refs)
    take = lambda n: [refs.pop(0) for _ in range(n)]
    table, weights = take(2)
    sources = take(len(shifts))
    corr, start_in, acc, xbuf = take(4)
    carry_over(start_in, acc)
    add_couplings(table, weights, at, "j", sign, shifts, sources, number, corr, xbuf, acc)


def last_kernel(*refs, at, sign, shifts, number, sizes_i, sizes_j, second):
    refs = list(refs)
    take = lambda n: [refs.pop(0) for _ in range(n)]
    table, weights = take(2)
    if not second:
        (incoming,) = take(1)
    (energy,) = take(1)
    sources = take(len(shifts))
    corr, start_in = take(2)
    if second:
        amp_in, residual_out, amp_out, acc, ebuf, xbuf, osem, psem = take(8)
    else:
        (acc,) = take(1)
        sends_i, sends_j = take(sizes_i[0]), take(sizes_j[0])
        ebuf, xbuf = take(2)
    pairs, width = acc.shape[0], acc.shape[1]
    carry_over(start_in, acc)
    add_couplings(table, weights, at, "j", sign, shifts, sources, number, corr, xbuf, acc)

    def settle(group):
        for p in group:
            residual = jnp.where(pair_window(table[at["count"] + p], width), acc[p], 0.0)
            acc[p] = residual
            step = residual / pair_denominator(energy, p, weights[at["occ"] + p], width)
            ebuf[p] = amp_in[p] - step if second else step
        if second:
            for p in group:
                pltpu.make_async_copy(acc.at[p], residual_out.at[p], osem.at[p]).start()
                pltpu.make_async_copy(ebuf.at[p], amp_out.at[p], psem.at[p]).start()

    grouped(pairs, settle)
    if not second:

        fill_sends(sizes_j[1], incoming, 0, ebuf, sends_j)
        fill_sends(sizes_i[1], incoming, sizes_j[0], ebuf, sends_i)
    else:

        def wait_out(p, carry):
            pltpu.make_async_copy(acc.at[p], residual_out.at[p], osem.at[p]).wait()
            pltpu.make_async_copy(ebuf.at[p], amp_out.at[p], psem.at[p]).wait()
            return carry

        lax.fori_loop(0, pairs, wait_out, 0)


def scratch_bytes(scratch):
    total = 0
    for ref in scratch:
        if ref.memory_space == pltpu.MemorySpace.VMEM:
            total += math.prod(ref.shape) * jnp.dtype(ref.dtype).itemsize
    return total


def call(kernel, outs, specs, scratch, args, flops, moved, out_specs=None, aliases=None):
    return pl.pallas_call(
        kernel,
        out_shape=outs,
        in_specs=specs,
        out_specs=out_specs or [VMEM] * len(outs),
        scratch_shapes=scratch,
        input_output_aliases=aliases or {},
        compiler_params=pltpu.CompilerParams(
            vmem_limit_bytes=scratch_bytes(scratch) + (6 << 20), flags=FLAGS
        ),
        cost_estimate=pl.CostEstimate(flops=flops, bytes_accessed=moved, transcendentals=0),
    )(*args)


def exchange(x, axis, k):
    size = lax.axis_size(axis)
    return lax.ppermute(x, axis, [(s, s ^ k) for s in range(size)])


def spread_rows(own, axis):
    size = lax.axis_size(axis)
    blocks = {0: own}
    low_bit = lambda k: k & -k
    top_bit = lambda k: 1 << (k.bit_length() - 1)
    bit = size // 2
    while bit:
        blocks[bit] = exchange(own, axis, bit)
        bit //= 2
    rest = [k for k in range(size) if k not in blocks]
    for k in sorted(rest, key=lambda k: (bin(k).count("1"), -k)):
        step = low_bit(k) if k >= size // 2 else top_bit(k)
        blocks[k] = exchange(blocks[k ^ step], axis, step)
    return [blocks[k] for k in range(size)]


def local(
    factors,
    pno_vecs,
    pair_occ,
    pno_count,
    pno_energy,
    occ_energy,
    coupi_peer,
    coupi_slot,
    coupi_target,
    coupi_fock,
    coupi_correlation,
    coupj_peer,
    coupj_slot,
    coupj_target,
    coupj_fock,
    coupj_correlation,
):
    size_i, size_j = lax.axis_size("occi"), lax.axis_size("occj")
    owned, aux, virs = factors.shape
    pairs, _, width = pno_vecs.shape
    number_i, number_j = coupi_slot.shape[0], coupj_slot.shape[0]
    dma = pltpu.SemaphoreType.DMA

    lists = jnp.stack([coupi_peer[:, 0], coupi_slot, coupj_peer[:, 0], coupj_slot]).astype(F32)
    lists = jnp.pad(lists, ((0, 4), (0, virs - number_i)), constant_values=-1.0)
    own = jnp.concatenate([factors, jnp.broadcast_to(lists, (owned,) + lists.shape)], axis=1)
    rows = spread_rows(own, "occj")
    columns = [own] + [exchange(own, "occi", k) for k in range(1, size_i)]

    cap_i = max(2, 2 * number_i // size_i)
    cap_j = max(2, 2 * number_j // size_j)
    sizes_i, sizes_j = (size_i, cap_i), (size_j, cap_j)
    crossing = list(range(size_j // 2, size_j))
    issue_j = crossing + list(range(1, size_j // 2))
    middle = [k for k in issue_j if k != size_j - 1]
    final = [size_j - 1]
    process_j = middle + final + [0]
    process_i = list(range(1, size_i)) + [0]
    rank_j = [process_j.index(k) for k in range(size_j)]
    rank_i = [process_i.index(k) for k in range(size_i)]
    at, top = {}, 0
    for name, length in (
        ("me", 2), ("order", pairs), ("row", pairs), ("col", pairs), ("count", pairs),
        ("start", size_j), ("counts", size_j), ("cursor", size_j),
        ("order_i", number_i), ("target_i", number_i),
        ("start_i", size_i), ("counts_i", size_i), ("cursor_i", size_i),
        ("order_j", number_j), ("target_j", number_j),
        ("start_j", size_j), ("counts_j", size_j), ("cursor_j", size_j),
    ):
        at[name] = top
        top += length
    at["occ"], at["fock_i"], at["fock_j"] = 0, pairs, pairs + number_i
    ints = lambda n: jax.ShapeDtypeStruct((n,), jnp.int32)
    index_args = [
        pair_occ[:, 0], pair_occ[:, 1], pno_count, coupi_peer[:, 0], coupi_target, coupi_fock,
        coupj_peer[:, 0], coupj_target, coupj_fock, occ_energy]
    index_args = [pltpu.with_memory_space_constraint(x, pltpu.HBM) for x in index_args]
    table, weights = call(
        functools.partial(
            index_kernel, at=at, owned=owned, rank_i=rank_i, rank_j=rank_j),
        [ints(top), jax.ShapeDtypeStruct((pairs + number_i + number_j,), F32)],
        [HBM] * 10,
        [pltpu.SMEM(x.shape, x.dtype) for x in index_args] + [dma((10,))],
        index_args,
        10000, 4096, out_specs=[SMEM] * 2)
    pair_shape = jax.ShapeDtypeStruct((pairs, width, width), F32)
    pair_buf = pltpu.VMEM((pairs, width, width), F32)
    sends = [jax.ShapeDtypeStruct((cap_i, width, width), F32)] * size_i
    sends += [jax.ShapeDtypeStruct((cap_j, width, width), F32)] * size_j
    pair_bytes = 4 * pairs * width * width

    pinned = lambda *xs: [pltpu.with_memory_space_constraint(x, pltpu.HBM) for x in xs]
    cuts = [0, size_j * 3 // 8, size_j * 3 // 4, size_j]
    state = []
    for low, high in zip(cuts[:-1], cuts[1:]):
        first, last = low == 0, high == size_j
        blocks = high - low
        cells = blocks * size_i * owned * owned
        args = [table, weights] + pinned(pno_energy, pno_vecs)
        args += rows[low:high] + columns
        if last:
            args += rows[:low]
        specs = [SMEM] * 2 + [HBM] * 2 + [VMEM] * (len(args) - 4)
        aliases = {}
        if not first:
            aliases = {len(args): 0, len(args) + 1: 1}
            args += state
            specs += [HBM] * 2
        scratch = [
            pair_buf,
            pair_buf,
            pltpu.VMEM((pairs, virs, width), F32),
            pltpu.VMEM(pno_energy.shape, F32),
            pltpu.VMEM((size_i * owned, 3 * aux, virs), BF16),
            pltpu.VMEM((cells, virs, virs), BF16),
            pltpu.VMEM((cells, virs, virs), BF16),
            dma((pairs,)),
            dma((1,)),
            dma((pairs,)),
            dma((pairs,)),
        ]
        outs = [pltpu.HBM(pair_shape.shape, F32)] * 2
        out_specs = [HBM] * 2
        if last:
            several = (size_i + size_j + 7) // 8 * 8
            outs += [jax.ShapeDtypeStruct((several, 128), jnp.int32)] + sends
            out_specs += [SMEM] + [VMEM] * len(sends)
            scratch += [pltpu.VMEM((several, 128), F32)] * 2 + [pltpu.VMEM((several, 128), jnp.int32), dma((1,))]
        kernel = functools.partial(
            integral_kernel, at=at, low=low, high=high, columns=size_i, owned=owned, aux=aux,
            first=first, last=last, sizes_i=sizes_i, sizes_j=sizes_j)
        share = blocks / size_j
        results = call(
            kernel, outs, specs, scratch, args,
            int(share * 6 * virs * (2 * size_j * size_i * aux * virs + pairs * 2 * width * (virs + width))),
            int(share * 4 * pairs * width * (virs + 2 * width) + 4 * (blocks + size_i) * aux * virs),
            out_specs, aliases)
        state = list(results[:2])
    amplitude, held = state
    incoming, sent = results[2], results[3:]

    up = lambda n: (n + CHUNK - 1) // CHUNK * CHUNK
    matrix = lambda n: pltpu.VMEM((up(n), width, width), F32)
    for iteration in range(2):
        again = iteration == 1
        sign = 1.0 if again else -1.0
        sent_i, sent_j = sent[:size_i], sent[size_i:]
        got_j = {k: exchange(sent_j[k], "occj", k) for k in issue_j}
        got_i = {k: exchange(sent_i[k], "occi", k) for k in range(1, size_i)}
        got_i[0], got_j[0] = sent_i[0], sent_j[0]

        args = [table, weights, pno_energy, got_j[0]] + [got_i[k] for k in process_i]
        args += [coupi_correlation, coupj_correlation]
        specs = [SMEM] * 2 + [VMEM] * (len(args) - 2)
        args += ([held] + pinned(amplitude)) if again else pinned(held)
        specs += [VMEM, HBM] if again else [HBM]
        results = call(
            functools.partial(
                near_kernel, at=at, sign=sign, shifts_i=process_i, number_i=number_i, number_j=number_j, second=again),
            [pair_shape] * (2 if again else 1), specs, [matrix(max(number_i, cap_j)), dma((1,))], args,
            12 * number_i * width**3, 2 * pair_bytes + 8 * number_i * width * width)
        partial = results[0]
        if again:
            amplitude = results[1]

        args = [table, weights] + [got_j[k] for k in middle] + [coupj_correlation, partial]
        (partial,) = call(
            functools.partial(middle_kernel, at=at, sign=sign, shifts=middle, number=number_j),
            [pair_shape], [SMEM] * 2 + [VMEM] * (len(args) - 2), [matrix(number_j)], args,
            12 * number_j * width**3, 2 * pair_bytes + 8 * number_j * width * width)

        args = [table, weights]
        if not again:
            args += [incoming]
        specs = [SMEM] * len(args)
        args += [pno_energy] + [got_j[k] for k in final] + [coupj_correlation, partial]
        outs, out_specs = [pair_shape], [VMEM]
        few = up(min(number_j, cap_j * len(final)))
        if again:
            args += [amplitude]
            outs, out_specs = [pair_shape] * 2, [HBM] * 2
            scratch = [pair_buf, pair_buf, matrix(few), dma((pairs,)), dma((pairs,))]
        else:
            outs, out_specs = [pair_shape] + sends, [VMEM] * (1 + len(sends))
            scratch = [pair_buf, matrix(few)]
        specs += [VMEM] * (len(args) - len(specs))
        results = call(
            functools.partial(
                last_kernel, at=at, sign=sign, shifts=final, number=number_j,
                sizes_i=sizes_i, sizes_j=sizes_j, second=again),
            outs, specs, scratch, args,
            12 * few * width**3, 3 * pair_bytes + 8 * few * width * width, out_specs)
        if again:
            residual, amplitude = results
        else:
            held, sent = results[0], results[1:]
    return amplitude, residual


def solution(mesh):
    lead = ("occi", "occj")
    placed = (
        P(lead, None, None),
        P(lead, None, None),
        P(lead, None),
        P(lead),
        P(lead, None),
        P(),
        P(lead, None),
        P(lead),
        P(lead),
        P(lead),
        P(lead, None, None),
        P(lead, None),
        P(lead),
        P(lead),
        P(lead),
        P(lead, None, None),
    )
    return jax.shard_map(
        local,
        mesh=mesh,
        in_specs=placed,
        out_specs=(P(lead, None, None), P(lead, None, None)),
        check_vma=False,
    )
```

```python
import functools
import math

import jax
import jax.numpy as jnp
from jax import lax
from jax.experimental import pallas as pl
from jax.experimental.pallas import tpu as pltpu
from jax.sharding import PartitionSpec as P


BATCH = 8
CHUNK = 4
SETTLE = 4
FLAGS = {}
ANY = pl.BlockSpec(memory_space=pl.ANY)
SMEM = pl.BlockSpec(memory_space=pltpu.SMEM)
VMEM = pl.BlockSpec(memory_space=pltpu.VMEM)
HBM = pl.BlockSpec(memory_space=pltpu.HBM)
F32 = jnp.float32
BF16 = jnp.bfloat16


def split(x):
    lead = x.astype(BF16)
    return lead, (x - lead.astype(F32)).astype(BF16)


def wide_left(x):
    lead, rest = split(x)
    return jnp.concatenate([lead, lead, rest], axis=1)


def wide_right(x, axis):
    lead, rest = split(x)
    return jnp.concatenate([lead, rest, lead], axis=axis)


def dot_nn(left, right):
    return lax.dot_general(left, right, (((1,), (0,)), ((), ())), preferred_element_type=F32)


def dot_nt(left, right):
    return lax.dot_general(left, right, (((1,), (1,)), ((), ())), preferred_element_type=F32)


def pair_window(count, width):
    row = lax.broadcasted_iota(jnp.int32, (width, width), 0)
    column = lax.broadcasted_iota(jnp.int32, (width, width), 1)
    return (row < count) & (column < count)


def pair_denominator(energy_ref, p, occ_sum, width):
    energies = jnp.broadcast_to(energy_ref[pl.ds(p, 1), :], (width, width))
    return energies + energies.T - occ_sum


def index_kernel(
    *refs, at, owned, rank_i, rank_j, rank_row
):
    inputs, (table, weights), local, sem = refs[:10], refs[10:12], refs[12:22], refs[22]
    copies = [pltpu.make_async_copy(inputs[n], local[n], sem.at[n]) for n in range(10)]
    for copy in copies:
        copy.start()
    for copy in copies:
        copy.wait()
    first, second, count, peer_i, target_i, fock_i, peer_j, target_j, fock_j, energy = local
    me_i, me_j = lax.axis_index("occi"), lax.axis_index("occj")
    size_i, size_j = len(rank_i), len(rank_j)
    table[at["me"]] = me_i
    table[at["me"] + 1] = me_j
    pairs = first.shape[0]

    def sort(number, size, rank, key, start, counts, cursor, place):
        for k in range(size):
            table[counts + k] = 0

        def tally(c, carry):
            table[counts + key(c)] += 1
            return carry

        lax.fori_loop(0, number, tally, 0)
        total = 0
        for k in sorted(range(size), key=lambda k: rank[k]):
            table[start + k] = total
            table[cursor + k] = total
            total = total + table[counts + k]

        def settle(c, carry):
            k = key(c)
            e = table[cursor + k]
            table[cursor + k] = e + 1
            place(c, k, e)
            return carry

        lax.fori_loop(0, number, settle, 0)

    def place_pair(p, k, e):
        table[at["order"] + e] = p

    def shift_of_pair(p):
        return ((first[p] - me_i * (owned * size_j)) // owned) ^ me_j

    for k in range(size_j):
        table[at["place"] + k] = rank_row[k]
    sort(pairs, size_j, rank_row, shift_of_pair, at["start"], at["counts"], at["cursor"], place_pair)

    def describe(p, carry):
        one, two = first[p], second[p]
        table[at["row"] + p] = table[at["place"] + shift_of_pair(p)] * owned + one % owned
        table[at["col"] + p] = ((two // owned // size_j) ^ me_i) * owned + two % owned
        weights[at["occ"] + p] = energy[one] + energy[two]
        table[at["count"] + p] = count[p]
        return carry

    lax.fori_loop(0, pairs, describe, 0)

    def one_list(name, peer, target, fock, me, size, rank):
        def place(c, k, e):
            table[at["order_" + name] + e] = c
            table[at["target_" + name] + e] = target[c]
            weights[at["fock_" + name] + e] = fock[c]

        sort(peer.shape[0], size, rank, lambda c: peer[c] ^ me, at["start_" + name], at["counts_" + name],
             at["cursor_" + name], place)

    one_list("i", peer_i, target_i, fock_i, me_i, size_i, rank_i)
    one_list("j", peer_j, target_j, fock_j, me_j, size_j, rank_j)


def read_requests(peer_ref, slot_ref, mine, caps, requests):
    lists, lanes = requests.shape
    lane = lax.broadcasted_iota(jnp.int32, (lists, lanes), 1)
    match = peer_ref[...] == mine
    ones = match.astype(F32)
    ahead = lax.broadcasted_iota(jnp.int32, (lanes, lanes), 0) < lax.broadcasted_iota(jnp.int32, (lanes, lanes), 1)
    place = dot_nn(ones.astype(BF16), ahead.astype(F32).astype(BF16))
    rows = jnp.where(lane == 127, jnp.sum(ones, axis=1, keepdims=True), 0.0)
    for r in range(caps):
        here = jnp.where(match & (place == r), slot_ref[...], 0.0)
        rows = jnp.where(lane == r, jnp.sum(here, axis=1, keepdims=True), rows)
    requests[...] = rows.astype(jnp.int32)


def fill_sends(cap, incoming, first, row_of, sends):
    step = math.gcd(cap, 4)
    for k, send in enumerate(sends):
        n = first + k

        def some(g, carry, send=send, n=n):
            for j in range(step):
                send[g * step + j] = row_of(incoming[n, g * step + j])
            return carry

        lax.fori_loop(0, jnp.minimum((incoming[n, 127] + step - 1) // step, cap // step), some, 0)


def integral_kernel(*refs, at, low, high, shifts, columns, owned, aux, first, last, sizes_i, sizes_j):
    refs = list(refs)
    take = lambda n: [refs.pop(0) for _ in range(n)]
    blocks = high - low
    table, weights = take(2)
    energy_in, vectors = take(2)
    row_blocks, col_blocks = take(blocks), take(columns)
    if last:
        others = take(low)
    if not first:
        old_amp, _ = take(2)
    amp_out, base_out = take(2)
    if last:
        (incoming,) = take(1)
        sends_i, sends_j = take(sizes_i[0]), take(sizes_j[0])
    amp, base, qbuf, energy, ccat, lead, rest, qsem, esem, asem, bsem = take(11)
    if last:
        peer_buf, slot_buf, requests, rsem = take(4)
    pairs, width = amp.shape[0], amp.shape[1]
    start = table[at["start"] + shifts[low]]
    stop = table[at["start"] + shifts[high]] if high < sizes_j[0] else pairs
    pltpu.make_async_copy(energy_in, energy, esem.at[0]).start()

    def load(t, carry):
        pltpu.make_async_copy(vectors.at[table[at["order"] + t]], qbuf.at[t], qsem.at[t]).start()
        return carry

    lax.fori_loop(start, stop, load, 0)
    if last:

        def load_old(t, carry):
            p = table[at["order"] + t]
            pltpu.make_async_copy(old_amp.at[p], amp.at[p], asem.at[t]).start()
            return carry

        lax.fori_loop(0, start, load_old, 0)
        by_place = others + row_blocks
        sources = [(by_place[shifts.index(k)], 2) for k in range(sizes_j[0])] + [(block, 0) for block in col_blocks]
        peer_buf[...] = jnp.full(peer_buf.shape, -1.0, F32)
        slot_buf[...] = jnp.zeros(slot_buf.shape, F32)
        for n, (block, row) in enumerate(sources):
            peer_buf[n : n + 1] = block[0, aux + row : aux + row + 1, :128]
            slot_buf[n : n + 1] = block[0, aux + row + 1 : aux + row + 2, :128]
        along_j = lax.broadcasted_iota(jnp.int32, peer_buf.shape, 0) < sizes_j[0]
        mine = jnp.where(along_j, table[at["me"] + 1], table[at["me"]]).astype(F32)
        read_requests(peer_buf, slot_buf, mine, max(sizes_i[1], sizes_j[1]), requests)
        tell = pltpu.make_async_copy(requests, incoming, rsem.at[0])
        tell.start()
    order = lambda t: table[at["order"] + t]
    ncol = columns * owned
    for b in range(columns):
        for o in range(owned):
            ccat[b * owned + o] = wide_right(col_blocks[b][o, :aux], 0)
    for b in range(blocks):
        for o in range(owned):
            left = wide_left(row_blocks[b][o, :aux].T)

            cell = (b * owned + o) * ncol
            step = math.gcd(ncol, 4)

            def column(g, carry, left=left, cell=cell, step=step):
                for c in range(step):
                    top, rem = split(dot_nn(left, ccat[g * step + c]))
                    lead[cell + g * step + c] = top
                    rest[cell + g * step + c] = rem
                return carry

            lax.fori_loop(0, ncol // step, column, 0)

    pltpu.make_async_copy(energy_in, energy, esem.at[0]).wait()

    def batch(head, size):
        for j in range(size):

            @pl.when(head + j < stop)
            def _(j=j):
                pltpu.make_async_copy(vectors.at[0], qbuf.at[head + j], qsem.at[head + j]).wait()

        results = []
        for j in range(size):
            t = jnp.minimum(head + j, stop - 1)
            p = order(t)
            q = qbuf[t]
            cell = (table[at["row"] + p] - low * owned) * ncol + table[at["col"] + p]
            top, rem = lead[cell], rest[cell]
            half = dot_nn(wide_left(q.T), jnp.concatenate([top, rem, top], axis=0))
            integral = dot_nn(wide_left(half), wide_right(q, 0))
            results.append((p, integral))
        for j in range(size):
            p, integral = results[j]
            integral = jnp.where(pair_window(table[at["count"] + p], width), integral, 0.0)
            denominator = pair_denominator(energy, p, weights[at["occ"] + p], width)
            amplitude = -integral / denominator
            amp[p] = amplitude
            base[p] = integral + denominator * amplitude
        for j in range(size):

            @pl.when(head + j < stop)
            def _(j=j):
                p = order(head + j)
                pltpu.make_async_copy(amp.at[p], amp_out.at[p], asem.at[head + j]).start()
                pltpu.make_async_copy(base.at[p], base_out.at[p], bsem.at[head + j]).start()

    def whole(g, carry):
        batch(start + g * BATCH, BATCH)
        return carry

    def part(g, carry):
        batch(start + many * BATCH + g * (BATCH // 2), BATCH // 2)
        return carry

    many = (stop - start) // BATCH
    lax.fori_loop(0, many, whole, 0)
    lax.fori_loop(0, (stop - start - many * BATCH + BATCH // 2 - 1) // (BATCH // 2), part, 0)
    if last:

        def wait_old(t, carry):
            pltpu.make_async_copy(old_amp.at[0], amp.at[0], asem.at[t]).wait()
            return carry

        lax.fori_loop(0, start, wait_old, 0)
        tell.wait()
        fill_sends(sizes_j[1], incoming, 0, lambda p: amp[p], sends_j)
        fill_sends(sizes_i[1], incoming, sizes_j[0], lambda p: amp[p], sends_i)

    def wait_out(t, carry):
        p = order(t)
        pltpu.make_async_copy(amp.at[p], amp_out.at[p], asem.at[t]).wait()
        pltpu.make_async_copy(base.at[p], base_out.at[p], bsem.at[t]).wait()
        return carry

    lax.fori_loop(start, stop, wait_out, 0)


def add_couplings(table, weights, at, name, sign, shifts, sources, number, correlation, xbuf, acc):
    first = table[at["start_" + name] + shifts[0]]
    used = 0
    for k, source in zip(shifts, sources):
        here = table[at["counts_" + name] + k]

        def one(r, carry, source=source, base=used):
            xbuf[base + r] = source[r]
            return carry

        lax.fori_loop(0, here, one, 0)
        used = used + here
    groups = (used + CHUNK - 1) // CHUNK

    def clear(e, carry):
        xbuf[e] = jnp.zeros(xbuf.shape[1:], F32)
        return carry

    lax.fori_loop(used, groups * CHUNK, clear, 0)

    def chunk(g, carry):
        terms = []
        for j in range(CHUNK):
            e = g * CHUNK + j
            matrix = correlation[table[at["order_" + name] + jnp.minimum(first + e, number - 1)]]
            top, low = split(matrix)
            half = dot_nn(jnp.concatenate([top, top, low], axis=1), wide_right(xbuf[e], 0))
            terms.append(dot_nt(wide_left(half), jnp.concatenate([top, low, top], axis=1)))
        for j in range(CHUNK):
            e = g * CHUNK + j
            s = jnp.minimum(first + e, number - 1)
            weight = jnp.where(e < used, sign * weights[at["fock_" + name] + s], 0.0)
            acc[table[at["target_" + name] + s]] += weight * terms[j]
        return carry

    lax.fori_loop(0, groups, chunk, 0)


def grouped(number, step):
    size = math.gcd(number, SETTLE)

    def some(g, carry):
        step([g * size + j for j in range(size)])
        return carry

    lax.fori_loop(0, number // size, some, 0)


def near_kernel(*refs, at, sign, shifts_i, number_i, number_j, second):
    refs = list(refs)
    take = lambda n: [refs.pop(0) for _ in range(n)]
    table, weights = take(2)
    (energy,) = take(1)
    (own_j,) = take(1)
    sources_i = take(len(shifts_i))
    corr_i, corr_j = take(2)
    (start_in,) = take(1)
    if second:
        inverse, amp_in, acc, amp, xbuf, sem = take(6)
    else:
        acc, inverse, xbuf, sem = take(4)
    pairs, width = acc.shape[0], acc.shape[1]
    fetch = pltpu.make_async_copy(amp_in if second else start_in, amp if second else acc, sem.at[0])
    fetch.start()
    if second:
        fetch.wait()

    def prepare(group):
        for p in group:
            window = pair_window(table[at["count"] + p], width)
            denominator = pair_denominator(energy, p, weights[at["occ"] + p], width)
            if second:
                residual = jnp.where(window, start_in[p], 0.0)
                step = start_in[p] * inverse[p]
                amp[p] = amp[p] - step
                acc[p] = residual - denominator * step
            else:
                inverse[p] = jnp.where(window, 1.0 / denominator, 0.0)

    grouped(pairs, prepare)
    if not second:
        fetch.wait()
    add_couplings(table, weights, at, "i", sign, shifts_i, sources_i, number_i, corr_i, xbuf, acc)
    add_couplings(table, weights, at, "j", sign, [0], [own_j], number_j, corr_j, xbuf, acc)


def carry_over(source, acc):
    def some(group):
        for p in group:
            acc[p] = source[p]

    grouped(acc.shape[0], some)


def middle_kernel(*refs, at, sign, shifts, number):
    refs = list(refs)
    take = lambda n: [refs.pop(0) for _ in range(n)]
    table, weights = take(2)
    sources = take(len(shifts))
    corr, start_in, acc, xbuf = take(4)
    carry_over(start_in, acc)
    add_couplings(table, weights, at, "j", sign, shifts, sources, number, corr, xbuf, acc)


def last_kernel(*refs, at, sign, shifts, number, sizes_i, sizes_j, second):
    refs = list(refs)
    take = lambda n: [refs.pop(0) for _ in range(n)]
    table, weights = take(2)
    if not second:
        (incoming,) = take(1)
    sources = take(len(shifts))
    corr, inverse, start_in = take(3)
    if second:
        amp_in, residual_out, amp_out, acc, ebuf, xbuf, osem, psem = take(8)
    else:
        (acc,) = take(1)
        sends_i, sends_j = take(sizes_i[0]), take(sizes_j[0])
        (xbuf,) = take(1)
    pairs, width = acc.shape[0], acc.shape[1]
    carry_over(start_in, acc)
    add_couplings(table, weights, at, "j", sign, shifts, sources, number, corr, xbuf, acc)
    if not second:
        step = lambda p: acc[p] * inverse[p]
        fill_sends(sizes_j[1], incoming, 0, step, sends_j)
        fill_sends(sizes_i[1], incoming, sizes_j[0], step, sends_i)
        return

    def settle(group):
        for p in group:
            residual = acc[p]
            ebuf[p] = amp_in[p] - residual * inverse[p]
            acc[p] = jnp.where(pair_window(table[at["count"] + p], width), residual, 0.0)
        for p in group:
            pltpu.make_async_copy(acc.at[p], residual_out.at[p], osem.at[p]).start()
            pltpu.make_async_copy(ebuf.at[p], amp_out.at[p], psem.at[p]).start()

    def wait_out(p, carry):
        pltpu.make_async_copy(acc.at[p], residual_out.at[p], osem.at[p]).wait()
        pltpu.make_async_copy(ebuf.at[p], amp_out.at[p], psem.at[p]).wait()
        return carry

    grouped(pairs, settle)
    lax.fori_loop(0, pairs, wait_out, 0)


def scratch_bytes(scratch):
    total = 0
    for ref in scratch:
        if ref.memory_space == pltpu.MemorySpace.VMEM:
            total += math.prod(ref.shape) * jnp.dtype(ref.dtype).itemsize
    return total


def call(kernel, outs, specs, scratch, args, flops, moved, out_specs=None, aliases=None):
    return pl.pallas_call(
        kernel,
        out_shape=outs,
        in_specs=specs,
        out_specs=out_specs or [VMEM] * len(outs),
        scratch_shapes=scratch,
        input_output_aliases=aliases or {},
        compiler_params=pltpu.CompilerParams(
            vmem_limit_bytes=scratch_bytes(scratch) + (6 << 20), flags=FLAGS
        ),
        cost_estimate=pl.CostEstimate(flops=flops, bytes_accessed=moved, transcendentals=0),
    )(*args)


def exchange(x, axis, k):
    size = lax.axis_size(axis)
    return lax.ppermute(x, axis, [(s, s ^ k) for s in range(size)])


def spread_rows(own, axis):
    size = lax.axis_size(axis)
    blocks = {0: own}
    low_bit = lambda k: k & -k
    top_bit = lambda k: 1 << (k.bit_length() - 1)
    bit = size // 2
    while bit:
        blocks[bit] = exchange(own, axis, bit)
        bit //= 2
    rest = [k for k in range(size) if k not in blocks]
    for k in sorted(rest, key=lambda k: (bin(k).count("1"), -k)):
        step = low_bit(k) if k >= size // 2 else top_bit(k)
        blocks[k] = exchange(blocks[k ^ step], axis, step)
    return [blocks[k] for k in range(size)]


def local(
    factors,
    pno_vecs,
    pair_occ,
    pno_count,
    pno_energy,
    occ_energy,
    coupi_peer,
    coupi_slot,
    coupi_target,
    coupi_fock,
    coupi_correlation,
    coupj_peer,
    coupj_slot,
    coupj_target,
    coupj_fock,
    coupj_correlation,
):
    size_i, size_j = lax.axis_size("occi"), lax.axis_size("occj")
    owned, aux, virs = factors.shape
    pairs, _, width = pno_vecs.shape
    number_i, number_j = coupi_slot.shape[0], coupj_slot.shape[0]
    dma = pltpu.SemaphoreType.DMA

    lists = jnp.stack([coupi_peer[:, 0], coupi_slot, coupj_peer[:, 0], coupj_slot]).astype(F32)
    lists = jnp.pad(lists, ((0, 4), (0, virs - number_i)), constant_values=-1.0)
    own = jnp.concatenate([factors, jnp.broadcast_to(lists, (owned,) + lists.shape)], axis=1)
    rows = spread_rows(own, "occj")
    columns = [own] + [exchange(own, "occi", k) for k in range(1, size_i)]

    cap_i = max(2, 2 * number_i // size_i)
    cap_j = max(2, 2 * number_j // size_j)
    sizes_i, sizes_j = (size_i, cap_i), (size_j, cap_j)
    crossing = list(range(size_j // 2, size_j))
    issue_j = crossing + list(range(1, size_j // 2))
    middle = [k for k in issue_j if k != size_j - 1]
    final = [size_j - 1]
    process_j = middle + final + [0]
    process_i = list(range(1, size_i)) + [0]
    rank_j = [process_j.index(k) for k in range(size_j)]
    rank_i = [process_i.index(k) for k in range(size_i)]
    third, half = size_j * 3 // 8, size_j // 2
    process_rows = list(range(third)) + list(range(half, size_j - 1)) + list(range(third, half)) + [size_j - 1]
    cuts = [0, third, third + half - 1, size_j]
    rank_row = [process_rows.index(k) for k in range(size_j)]
    at, top = {}, 0
    for name, length in (
        ("me", 2), ("place", size_j), ("order", pairs), ("row", pairs), ("col", pairs), ("count", pairs),
        ("start", size_j), ("counts", size_j), ("cursor", size_j),
        ("order_i", number_i), ("target_i", number_i),
        ("start_i", size_i), ("counts_i", size_i), ("cursor_i", size_i),
        ("order_j", number_j), ("target_j", number_j),
        ("start_j", size_j), ("counts_j", size_j), ("cursor_j", size_j),
    ):
        at[name] = top
        top += length
    at["occ"], at["fock_i"], at["fock_j"] = 0, pairs, pairs + number_i
    ints = lambda n: jax.ShapeDtypeStruct((n,), jnp.int32)
    index_args = [
        pair_occ[:, 0], pair_occ[:, 1], pno_count, coupi_peer[:, 0], coupi_target, coupi_fock,
        coupj_peer[:, 0], coupj_target, coupj_fock, occ_energy]
    index_args = [pltpu.with_memory_space_constraint(x, pltpu.HBM) for x in index_args]
    table, weights = call(
        functools.partial(
            index_kernel, at=at, owned=owned, rank_i=rank_i, rank_j=rank_j, rank_row=rank_row),
        [ints(top), jax.ShapeDtypeStruct((pairs + number_i + number_j,), F32)],
        [HBM] * 10,
        [pltpu.SMEM(x.shape, x.dtype) for x in index_args] + [dma((10,))],
        index_args,
        10000, 4096, out_specs=[SMEM] * 2)
    pair_shape = jax.ShapeDtypeStruct((pairs, width, width), F32)
    pair_buf = pltpu.VMEM((pairs, width, width), F32)
    sends = [jax.ShapeDtypeStruct((cap_i, width, width), F32)] * size_i
    sends += [jax.ShapeDtypeStruct((cap_j, width, width), F32)] * size_j
    pair_bytes = 4 * pairs * width * width

    pinned = lambda *xs: [pltpu.with_memory_space_constraint(x, pltpu.HBM) for x in xs]
    placed_rows = [rows[k] for k in process_rows]
    state = []
    for low, high in zip(cuts[:-1], cuts[1:]):
        first, last = low == 0, high == size_j
        blocks = high - low
        cells = blocks * size_i * owned * owned
        args = [table, weights] + pinned(pno_energy, pno_vecs)
        args += placed_rows[low:high] + columns
        if last:
            args += placed_rows[:low]
        specs = [SMEM] * 2 + [HBM] * 2 + [VMEM] * (len(args) - 4)
        aliases = {}
        if not first:
            aliases = {len(args): 0, len(args) + 1: 1}
            args += state
            specs += [HBM] * 2
        scratch = [
            pair_buf,
            pair_buf,
            pltpu.VMEM((pairs, virs, width), F32),
            pltpu.VMEM(pno_energy.shape, F32),
            pltpu.VMEM((size_i * owned, 3 * aux, virs), BF16),
            pltpu.VMEM((cells, virs, virs), BF16),
            pltpu.VMEM((cells, virs, virs), BF16),
            dma((pairs,)),
            dma((1,)),
            dma((pairs,)),
            dma((pairs,)),
        ]
        outs = [pltpu.HBM(pair_shape.shape, F32)] * 2
        out_specs = [HBM] * 2
        if last:
            several = (size_i + size_j + 7) // 8 * 8
            outs += [jax.ShapeDtypeStruct((several, 128), jnp.int32)] + sends
            out_specs += [SMEM] + [VMEM] * len(sends)
            scratch += [pltpu.VMEM((several, 128), F32)] * 2 + [pltpu.VMEM((several, 128), jnp.int32), dma((1,))]
        kernel = functools.partial(
            integral_kernel, at=at, low=low, high=high, shifts=process_rows, columns=size_i, owned=owned, aux=aux,
            first=first, last=last, sizes_i=sizes_i, sizes_j=sizes_j)
        share = blocks / size_j
        results = call(
            kernel, outs, specs, scratch, args,
            int(share * 6 * virs * (2 * size_j * size_i * aux * virs + pairs * 2 * width * (virs + width))),
            int(share * 4 * pairs * width * (virs + 2 * width) + 4 * (blocks + size_i) * aux * virs),
            out_specs, aliases)
        state = list(results[:2])
    amplitude, held = state
    incoming, sent = results[2], results[3:]

    up = lambda n: (n + CHUNK - 1) // CHUNK * CHUNK
    matrix = lambda n: pltpu.VMEM((up(n), width, width), F32)
    for iteration in range(2):
        again = iteration == 1
        sign = 1.0 if again else -1.0
        sent_i, sent_j = sent[:size_i], sent[size_i:]
        got_j = {k: exchange(sent_j[k], "occj", k) for k in issue_j}
        got_i = {k: exchange(sent_i[k], "occi", k) for k in range(1, size_i)}
        got_i[0], got_j[0] = sent_i[0], sent_j[0]

        args = [table, weights, pno_energy, got_j[0]] + [got_i[k] for k in process_i]
        args += [coupi_correlation, coupj_correlation]
        specs = [SMEM] * 2 + [VMEM] * (len(args) - 2)
        args += ([held, inverse] + pinned(amplitude)) if again else pinned(held)
        specs += [VMEM, VMEM, HBM] if again else [HBM]
        results = call(
            functools.partial(
                near_kernel, at=at, sign=sign, shifts_i=process_i, number_i=number_i, number_j=number_j, second=again),
            [pair_shape] * 2, specs, [matrix(max(number_i, cap_j)), dma((1,))], args,
            12 * number_i * width**3, 2 * pair_bytes + 8 * number_i * width * width)
        if again:
            partial, amplitude = results
        else:
            partial, inverse = results

        args = [table, weights] + [got_j[k] for k in middle] + [coupj_correlation, partial]
        (partial,) = call(
            functools.partial(middle_kernel, at=at, sign=sign, shifts=middle, number=number_j),
            [pair_shape], [SMEM] * 2 + [VMEM] * (len(args) - 2), [matrix(number_j)], args,
            12 * number_j * width**3, 2 * pair_bytes + 8 * number_j * width * width)

        args = [table, weights]
        if not again:
            args += [incoming]
        specs = [SMEM] * len(args)
        args += [got_j[k] for k in final] + [coupj_correlation, inverse, partial]
        outs, out_specs = [pair_shape], [VMEM]
        few = up(min(number_j, cap_j * len(final)))
        if again:
            args += [amplitude]
            outs, out_specs = [pair_shape] * 2, [HBM] * 2
            scratch = [pair_buf, pair_buf, matrix(few), dma((pairs,)), dma((pairs,))]
        else:
            outs, out_specs = [pair_shape] + sends, [VMEM] * (1 + len(sends))
            scratch = [matrix(few)]
        specs += [VMEM] * (len(args) - len(specs))
        results = call(
            functools.partial(
                last_kernel, at=at, sign=sign, shifts=final, number=number_j,
                sizes_i=sizes_i, sizes_j=sizes_j, second=again),
            outs, specs, scratch, args,
            12 * few * width**3, 3 * pair_bytes + 8 * few * width * width, out_specs)
        if again:
            residual, amplitude = results
        else:
            held, sent = results[0], results[1:]
    return amplitude, residual


def solution(mesh):
    lead = ("occi", "occj")
    placed = (
        P(lead, None, None),
        P(lead, None, None),
        P(lead, None),
        P(lead),
        P(lead, None),
        P(),
        P(lead, None),
        P(lead),
        P(lead),
        P(lead),
        P(lead, None, None),
        P(lead, None),
        P(lead),
        P(lead),
        P(lead),
        P(lead, None, None),
    )
    return jax.shard_map(
        local,
        mesh=mesh,
        in_specs=placed,
        out_specs=(P(lead, None, None), P(lead, None, None)),
        check_vma=False,
    )
```
